256 devices in a mesh: group: 16 (over y, x), dev: 16 (over z, core).
Axes of the slice: x: 4, y: 4, z: 8, core: 2. Of those that a mesh axis runs over, the one named last changes fastest.
Arguments:
- grid_state: bfloat16 [262144, 512], P(('group', 'dev')), may hold values from -6 to 6
- mesh_state: bfloat16 [32768, 512], P(('group', 'dev')), may hold values from -6 to 6
- encode_edge: bfloat16 [512, 512], replicated, may hold values from -0.25 to 0.25
- encode_first: bfloat16 [512, 512], replicated, may hold values from -0.25 to 0.25
- encode_second: bfloat16 [512, 512], replicated, may hold values from -0.25 to 0.25
- process_edge: bfloat16 [512, 512], replicated, may hold values from -0.25 to 0.25
- process_first: bfloat16 [512, 512], replicated, may hold values from -0.25 to 0.25
- process_second: bfloat16 [512, 512], replicated, may hold values from -0.25 to 0.25
- decode_edge: bfloat16 [512, 512], replicated, may hold values from -0.25 to 0.25
- decode_first: bfloat16 [512, 512], replicated, may hold values from -0.25 to 0.25
- decode_second: bfloat16 [512, 512], replicated, may hold values from -0.25 to 0.25
- encode_near: bfloat16 [3, 32768, 1024], P(None, ('group', 'dev')), may hold values from -0.09375 to 0.09375
- encode_live: int32 [3, 2048], P(None, ('group', 'dev')), may hold values 0 or 1
- encode_far: bfloat16 [2, 32768, 1024], P(None, ('group', 'dev')), may hold values from -0.09375 to 0.09375
- encode_groups: int32 [2, 256], P(None, ('group', 'dev')), may hold values from 0 to 15, as said below
- process_near: bfloat16 [3, 32768, 128], P(None, ('group', 'dev')), may hold values from -0.25 to 0.25
- process_far: bfloat16 [2, 32768, 128], P(None, ('group', 'dev')), may hold values from -0.25 to 0.25
- process_groups: int32 [2, 256], P(None, ('group', 'dev')), may hold values from 0 to 15, as said below
- decode_near: bfloat16 [3, 262144, 128], P(None, ('group', 'dev')), may hold values from -0.3125 to 0.3125
- decode_live: int32 [3, 2048], P(None, ('group', 'dev')), may hold values 0 or 1
Outputs:
- grid_next: bfloat16 [262144, 512], P(('group', 'dev'))
- mesh_next: bfloat16 [32768, 512], P(('group', 'dev'))
The draws below stay inside these ranges and needn't reach their ends.
Inputs may be any that keep to these rules, and one draw needn't show every extreme that they name: `encode_groups`: for each device q the 2 entries of column q are distinct regions, none equal to q's own region q // 16. `process_groups`: for each device q the 2 entries of column q are distinct regions, none equal to q's own region q // 16.
All inputs are finite; a program needn't handle non-finite values. No bound on the sum of `encode_live` or of `decode_live` on one device may be relied on, other than what follows from the above.
Results may differ from the reference program's by a relative error of at most 0.013.
Values may be sent and summed in bfloat16 or wider, within the bound.
No kernel may reach another device: no remote copies, remote signals or barrier semaphores. Data moves between devices by JAX's collectives and lax.ppermute only.
A program may use at most 64 MiB of HBM per device.

```python
import jax
import jax.numpy as jnp
from jax import lax

D = 512
TILE = 128
GRID_DEV = 1024
LONG = 2
TILES_DEV = 8
GRID_NODES = 262144
MESH_NODES = 32768
N_GROUP = 16
N_DEV = 16
DEVICES = 256


def far_regions(key):
    total_devices = N_GROUP * N_DEV
    scores = jax.random.randint(key, (total_devices, N_GROUP - 1), 0, 1 << 20) * N_GROUP
    scores = scores + jnp.arange(N_GROUP - 1, dtype=jnp.int32)[None, :]
    chosen = jnp.argsort(scores, axis=1, stable=True)[:, :LONG].astype(jnp.int32)
    own_group = jnp.arange(total_devices, dtype=jnp.int32) // N_DEV
    return ((own_group[:, None] + 1 + chosen) % N_GROUP).T.astype(jnp.int32)


def draw_encode_groups(key, part):
    return far_regions(jax.random.fold_in(key, 11))


def draw_process_groups(key, part):
    return far_regions(jax.random.fold_in(key, 23))


def place_ends(result, own_key, least, high):
    place = [jax.random.randint(jax.random.fold_in(own_key, axis), (), 0, length) for axis, length in enumerate(result.shape)]
    main_axis = result.shape.index(max(result.shape))
    next_to = place[:main_axis] + [(place[main_axis] + 1) % result.shape[main_axis]] + place[main_axis + 1:]
    return result.at[tuple(place)].set(least).at[tuple(next_to)].set(high)


def block_levels(own_key, extent, shards, smallest, largest):
    loudness, own = 1.0, jax.random.fold_in(own_key, 6)
    for axis_at, parts in shards:
        draws = jnp.exp(jax.random.uniform(jax.random.fold_in(own, axis_at), (parts,), jnp.float32, smallest / len(shards), largest / len(shards)))
        loudness = loudness * jnp.repeat(draws, extent[axis_at] // parts).reshape([-1 if axis == axis_at else 1 for axis in range(len(extent))])
    return loudness


def normal_values(stream_key, dims, spread, limit, pieces=(), kind=jnp.bfloat16):
    array = jax.random.normal(stream_key, dims, jnp.float32) * spread
    if len(pieces) > 0:
        array = block_levels(stream_key, dims, pieces, -0.22, 0.18) * array
    return jnp.clip(array, min=-limit, max=limit).astype(kind)


def setup_inputs(seed: int = 0) -> dict:
    key_of = jax.random.split(jax.random.key(seed), 21)
    return {
        "grid_state": normal_values(key_of[0], (GRID_NODES, D), 1.0, 6.0, ((0, 256),)),
        "mesh_state": normal_values(key_of[1], (MESH_NODES, D), 1.0, 6.0, ((0, 256),)),
        "encode_edge": normal_values(key_of[2], (D, D), D ** -0.5, 0.25),
        "encode_first": normal_values(key_of[3], (D, D), D ** -0.5, 0.25),
        "encode_second": normal_values(key_of[4], (D, D), D ** -0.5, 0.25),
        "process_edge": normal_values(key_of[5], (D, D), D ** -0.5, 0.25),
        "process_first": normal_values(key_of[6], (D, D), D ** -0.5, 0.25),
        "process_second": normal_values(key_of[7], (D, D), D ** -0.5, 0.25),
        "decode_edge": normal_values(key_of[8], (D, D), D ** -0.5, 0.25),
        "decode_first": normal_values(key_of[9], (D, D), D ** -0.5, 0.25),
        "decode_second": normal_values(key_of[10], (D, D), D ** -0.5, 0.25),
        "encode_near": normal_values(key_of[11], (3, MESH_NODES, GRID_DEV), (4 * GRID_DEV) ** -0.5, 0.09375, ((1, 256),)),
        "encode_live": place_ends((jax.random.randint(key_of[12], (3, TILES_DEV * DEVICES), 0, 3) < 2).astype(jnp.int32), jax.random.fold_in(key_of[12], 1), 0, 1),
        "encode_far": normal_values(key_of[13], (LONG, MESH_NODES, GRID_DEV), (4 * GRID_DEV) ** -0.5, 0.09375, ((1, 256),)),
        "encode_groups": draw_encode_groups(jax.random.fold_in(key_of[20], 71), 0),
        "process_near": normal_values(key_of[15], (3, MESH_NODES, TILE), (5 * TILE) ** -0.5, 0.25, ((1, 256),)),
        "process_far": normal_values(key_of[16], (LONG, MESH_NODES, TILE), (5 * TILE) ** -0.5, 0.25, ((1, 256),)),
        "process_groups": draw_process_groups(jax.random.fold_in(key_of[20], 71), 0),
        "decode_near": normal_values(key_of[18], (3, GRID_NODES, TILE), (3 * TILE) ** -0.5, 0.3125, ((1, 256),)),
        "decode_live": place_ends((jax.random.randint(key_of[19], (3, TILES_DEV * DEVICES), 0, 3) < 2).astype(jnp.int32), jax.random.fold_in(key_of[19], 1), 0, 1),
    }


highest = lax.Precision.HIGHEST

def layer_norm(row_values):
    row_mean = lax.optimization_barrier(jnp.mean(row_values, axis=-1, keepdims=True))
    centred = row_values - row_mean
    variance = lax.optimization_barrier(jnp.mean(centred * centred, axis=-1, keepdims=True))
    return centred * lax.rsqrt(variance + 1e-05)

def node_update(residual_in, summed, weight_in, weight_out):
    normed = layer_norm(summed).astype(jnp.bfloat16)
    hidden = jax.nn.silu(jnp.dot(normed, weight_in, preferred_element_type=jnp.float32)).astype(jnp.bfloat16)
    updated = residual_in.astype(jnp.float32) + jnp.dot(hidden, weight_out, preferred_element_type=jnp.float32)
    return updated.astype(jnp.bfloat16)

def edge_messages(latents, weight):
    return jax.nn.silu(jnp.dot(latents, weight, preferred_element_type=jnp.float32)).astype(jnp.bfloat16)

def shift_blocks(stacked):
    empty = jnp.zeros_like(stacked[:, :1])
    from_below = jnp.concatenate([empty, stacked[:, :-1]], axis=1)
    from_above = jnp.concatenate([stacked[:, 1:], empty], axis=1)
    return (from_below, from_above)

def reference(grid_state, mesh_state, encode_edge, encode_first, encode_second, process_edge, process_first, process_second, decode_edge, decode_first, decode_second, encode_near, encode_live, encode_far, encode_groups, process_near, process_far, process_groups, decode_near, decode_live):
    enc_msg = edge_messages(grid_state, encode_edge).reshape(N_GROUP, N_DEV, GRID_DEV, D)
    live_enc = encode_live.reshape(3, N_GROUP, N_DEV, TILES_DEV).transpose(1, 0, 2, 3)
    near_enc = encode_near.reshape(3, N_GROUP, N_DEV, TILE, GRID_DEV).transpose(1, 0, 2, 3, 4)
    far_enc = encode_far.reshape(LONG, N_GROUP, N_DEV, TILE, GRID_DEV).transpose(1, 0, 2, 3, 4)

    def group_sources(inputs):
        messages, live_flags, near_tiles, far_tiles = inputs
        wide = messages.astype(jnp.float32)
        near_out = []
        for offset in range(3):
            flags = jnp.repeat(live_flags[offset].astype(jnp.float32), TILE, axis=1)
            masked = wide * flags[:, :, None]
            product = jnp.einsum('dtr,drk->dtk', near_tiles[offset].astype(jnp.float32), masked, precision=highest)
            near_out.append(product.astype(jnp.bfloat16))
        far_out = []
        for index in range(LONG):
            product = jnp.einsum('dtr,drk->dtk', far_tiles[index].astype(jnp.float32), wide, precision=highest)
            far_out.append(product.astype(jnp.bfloat16))
        return (jnp.stack(near_out), jnp.stack(far_out))
    near_part, far_part = lax.map(group_sources, (enc_msg, live_enc, near_enc, far_enc))
    near_wide = near_part.astype(jnp.float32)
    from_below, from_above = shift_blocks(near_wide[:, 2])
    above_part = jnp.concatenate([near_wide[:, 0, 1:], jnp.zeros_like(near_wide[:, 0, :1])], axis=1)
    enc_sum = near_wide[:, 1] + from_below + above_part
    groups_enc = encode_groups.reshape(LONG, N_GROUP, N_DEV)
    select_enc = (groups_enc[..., None] == jnp.arange(N_GROUP, dtype=jnp.int32)).astype(jnp.float32)
    enc_sum = enc_sum + jnp.einsum('lgdh,gldtk->hdtk', select_enc, far_part.astype(jnp.float32), precision=highest)
    mesh_mid = node_update(mesh_state, enc_sum.reshape(MESH_NODES, D), encode_first, encode_second)
    proc_msg = edge_messages(mesh_mid, process_edge).reshape(N_GROUP, N_DEV, TILE, D).astype(jnp.float32)
    below_msg, above_msg = shift_blocks(proc_msg)
    near_proc = process_near.reshape(3, N_GROUP, N_DEV, TILE, TILE).astype(jnp.float32)
    proc_sum = jnp.einsum('gdij,gdjk->gdik', near_proc[0], below_msg, precision=highest)
    proc_sum = proc_sum + jnp.einsum('gdij,gdjk->gdik', near_proc[1], proc_msg, precision=highest)
    proc_sum = proc_sum + jnp.einsum('gdij,gdjk->gdik', near_proc[2], above_msg, precision=highest)
    groups_proc = process_groups.reshape(LONG, N_GROUP, N_DEV)
    select_proc = (groups_proc[..., None] == jnp.arange(N_GROUP, dtype=jnp.int32)).astype(jnp.float32)
    picked = jnp.einsum('lgdh,hdjk->lgdjk', select_proc, proc_msg, precision=highest)
    far_proc = process_far.reshape(LONG, N_GROUP, N_DEV, TILE, TILE).astype(jnp.float32)
    proc_sum = proc_sum + jnp.einsum('lgdij,lgdjk->gdik', far_proc, picked, precision=highest)
    mesh_next = node_update(mesh_mid, proc_sum.reshape(MESH_NODES, D), process_first, process_second)
    dec_msg = edge_messages(mesh_next, decode_edge).reshape(N_GROUP, N_DEV, TILE, D)
    dec_below, dec_above = shift_blocks(dec_msg)
    near_dec = decode_near.reshape(3, N_GROUP, N_DEV, GRID_DEV, TILE).transpose(1, 0, 2, 3, 4)
    live_dec = decode_live.reshape(3, N_GROUP, N_DEV, TILES_DEV).transpose(1, 0, 2, 3)
    grid_groups = grid_state.reshape(N_GROUP, N_DEV * GRID_DEV, D)

    def group_decode(inputs):
        below_blk, own_blk, above_blk, near_tiles, live_flags, grid_rows = inputs
        sources = (below_blk, own_blk, above_blk)
        summed = jnp.zeros((N_DEV, GRID_DEV, D), jnp.float32)
        for offset in range(3):
            product = jnp.einsum('dri,dik->drk', near_tiles[offset].astype(jnp.float32), sources[offset].astype(jnp.float32), precision=highest)
            flags = jnp.repeat(live_flags[offset].astype(jnp.float32), TILE, axis=1)
            summed = summed + product * flags[:, :, None]
        return node_update(grid_rows, summed.reshape(N_DEV * GRID_DEV, D), decode_first, decode_second)
    grid_next = lax.map(group_decode, (dec_below, dec_msg, dec_above, near_dec, live_dec, grid_groups))
    return (grid_next.reshape(GRID_NODES, D), mesh_next)
```

```python
import jax
import jax.numpy as jnp
from jax import lax
from jax.sharding import PartitionSpec as P


AXES = ("group", "dev")
LINE = 4


def line_pairs(axis_sizes, second, step):
    groups, devs = axis_sizes
    pairs = []
    for region in range(groups):
        y, x = divmod(region, LINE)
        for dev in range(devs):
            along_x = (dev % 2 == 0) != second
            other = y * LINE + (x ^ step) if along_x else (y ^ step) * LINE + x
            pairs.append((region * devs + dev, other * devs + dev))
    return pairs


def near_pairs(axis_sizes, odd):
    groups, devs = axis_sizes
    pairs = []
    for region in range(groups):
        for dev in range(odd, devs - 1, 2):
            low = region * devs + dev
            pairs += [(low, low + 1), (low + 1, low)]
    return pairs


def layer_norm(row_values):
    row_mean = jnp.mean(row_values, axis=-1, keepdims=True)
    centred = row_values - row_mean
    variance = jnp.mean(centred * centred, axis=-1, keepdims=True)
    return centred * lax.rsqrt(variance + 1e-05)


def dot(a, b):
    return jnp.dot(a, b, preferred_element_type=jnp.float32)


def node_update(residual_in, summed, weight_in, weight_out):
    normed = layer_norm(summed).astype(jnp.bfloat16)
    hidden = jax.nn.silu(dot(normed, weight_in)).astype(jnp.bfloat16)
    return (residual_in.astype(jnp.float32) + dot(hidden, weight_out)).astype(jnp.bfloat16)


def edge_messages(latents, weight):
    return jax.nn.silu(dot(latents, weight)).astype(jnp.bfloat16)


def body(
    grid_state,
    mesh_state,
    encode_edge,
    encode_first,
    encode_second,
    process_edge,
    process_first,
    process_second,
    decode_edge,
    decode_first,
    decode_second,
    encode_near,
    encode_live,
    encode_far,
    encode_groups,
    process_near,
    process_far,
    process_groups,
    decode_near,
    decode_live,
):
    f32, bf16 = jnp.float32, jnp.bfloat16
    sizes = (lax.axis_size("group"), lax.axis_size("dev"))
    rows, features = mesh_state.shape
    tiles = grid_state.shape[0] // rows
    region, dev = lax.axis_index("group"), lax.axis_index("dev")
    odd = dev % 2
    y, x = region // LINE, region % LINE
    first_at = jnp.where(odd == 0, x, y)
    second_at = jnp.where(odd == 0, y, x)

    def region_of(u, v):
        return jnp.where(odd == 0, v * LINE + u, u * LINE + v).astype(f32)

    def swap(value, second, step):
        return lax.ppermute(value, AXES, line_pairs(sizes, second, step))

    def near_swap(value, far_pair):
        return lax.ppermute(value, AXES, near_pairs(sizes, far_pair))

    at_a, at_b = 2 - 2 * odd, 2 * odd

    enc_msg = edge_messages(grid_state, encode_edge)
    far_parts = dot(encode_far.reshape(2 * rows, -1), enc_msg).astype(bf16)
    codes = jnp.concatenate([encode_groups[:, 0], process_groups[:, 0], jnp.zeros((12,), jnp.int32)])
    tags = jnp.broadcast_to(codes.astype(bf16)[:, None], (16, features))
    packet = jnp.concatenate([far_parts, tags], axis=0)
    packets = [packet] + [swap(packet, False, step) for step in (1, 2, 3)]

    stacked = enc_msg.reshape(tiles, rows, features)

    def near_part(index):
        live = encode_live[index].astype(bf16)
        masked = (stacked * live[:, None, None]).reshape(-1, features)
        return dot(encode_near[index], masked).astype(bf16)

    part_a = near_part(at_a)
    part_b = near_part(at_b)
    near_sum = near_part(1).astype(f32) + near_swap(part_a, 0).astype(f32) + near_swap(part_b, 1).astype(f32)

    def line_sum(v):
        code = region_of(first_at, v)
        total = jnp.zeros((rows, features), f32)
        for one in packets:
            for slot in range(2):
                hit = one[2 * rows + slot].astype(f32) == code
                total = total + jnp.where(hit[None], one[slot * rows : (slot + 1) * rows].astype(f32), 0.0)
        return total.astype(bf16)

    enc_sum = near_sum + line_sum(second_at).astype(f32)
    for step in (1, 2, 3):
        enc_sum = enc_sum + swap(line_sum(second_at ^ step), True, step).astype(f32)

    mesh_mid = node_update(mesh_state, enc_sum, encode_first, encode_second)
    proc_msg = edge_messages(mesh_mid, process_edge)

    column = [(second_at, proc_msg)] + [(second_at ^ step, swap(proc_msg, True, step)) for step in (1, 2, 3)]
    below_above = (near_swap(proc_msg, 0), near_swap(proc_msg, 1))
    proc_sum = dot(process_near[1], proc_msg)
    proc_sum = proc_sum + dot(process_near[at_a], below_above[0]) + dot(process_near[at_b], below_above[1])

    def wanted(one):
        slots = []
        for slot in range(2):
            want = one[2 * rows + 2 + slot].astype(f32)
            found = jnp.zeros((rows, features), bf16)
            for v, tile in column:
                found = jnp.where((want == region_of(first_at, v))[None], tile, found)
            slots.append(found)
        return jnp.concatenate(slots, axis=0)

    picked = wanted(packets[0]).astype(f32)
    for step in (1, 2, 3):
        picked = picked + swap(wanted(packets[step]), False, step).astype(f32)
    picked = picked.astype(bf16)
    for slot in range(2):
        proc_sum = proc_sum + dot(process_far[slot], picked[slot * rows : (slot + 1) * rows])
    mesh_next = node_update(mesh_mid, proc_sum, process_first, process_second)

    dec_msg = edge_messages(mesh_next, decode_edge)
    dec_sum = jnp.zeros((tiles, rows, features), f32)
    for index, source in ((1, dec_msg), (at_a, near_swap(dec_msg, 0)), (at_b, near_swap(dec_msg, 1))):
        product = dot(decode_near[index], source).reshape(tiles, rows, features)
        dec_sum = dec_sum + product * decode_live[index].astype(f32)[:, None, None]
    grid_next = node_update(grid_state, dec_sum.reshape(-1, features), decode_first, decode_second)
    return (grid_next, mesh_next)


def solution(mesh):
    split = P(AXES, None)
    inner = P(None, AXES, None)
    flags = P(None, AXES)
    return jax.shard_map(
        body,
        mesh=mesh,
        in_specs=(split, split) + (P(),) * 9 + (inner, flags, inner, flags, inner, inner, flags, inner, flags),
        out_specs=(split, split),
        check_vma=False,
    )
```

```python
import jax
import jax.numpy as jnp
from jax import lax
from jax.experimental import pallas as pl
from jax.experimental.pallas import tpu as pltpu
from jax.sharding import PartitionSpec as P


AXES = ("group", "dev")
LINE = 4


def line_pairs(axis_sizes, second, step):
    groups, devs = axis_sizes
    pairs = []
    for region in range(groups):
        y, x = divmod(region, LINE)
        for dev in range(devs):
            along_x = (dev % 2 == 0) != second
            other = y * LINE + (x ^ step) if along_x else (y ^ step) * LINE + x
            pairs.append((region * devs + dev, other * devs + dev))
    return pairs


def near_pairs(axis_sizes, odd):
    groups, devs = axis_sizes
    pairs = []
    for region in range(groups):
        for dev in range(odd, devs - 1, 2):
            low = region * devs + dev
            pairs += [(low, low + 1), (low + 1, low)]
    return pairs


F32, BF16 = jnp.float32, jnp.bfloat16
VMEM = pl.BlockSpec(memory_space=pltpu.VMEM)
SMEM = pl.BlockSpec(memory_space=pltpu.SMEM)
HBM = pl.BlockSpec(memory_space=pltpu.HBM)
CHUNK = 256


def dot(a, b):
    return jnp.dot(a, b, preferred_element_type=F32)


def silu(v):
    return v * (0.5 * jnp.tanh(0.5 * v) + 0.5)


def norm_rows(v):
    centred = v - jnp.mean(v, axis=-1, keepdims=True)
    variance = jnp.mean(centred * centred, axis=-1, keepdims=True)
    return (centred * lax.rsqrt(variance + 1e-05)).astype(BF16)


def parity():
    return lax.rem(lax.axis_index("dev"), 2)


def column_codes():
    region, odd = lax.axis_index("group"), parity()
    y, x = lax.div(region, LINE), lax.rem(region, LINE)
    first_at, second_at = jnp.where(odd == 0, x, y), jnp.where(odd == 0, y, x)
    scale_u, scale_v = jnp.where(odd == 0, 1, LINE), jnp.where(odd == 0, LINE, 1)
    return [(first_at * scale_u + lax.bitwise_xor(second_at, step) * scale_v).astype(F32) for step in range(LINE)]


def encode_far_kernel(enc_codes, proc_codes, grid_hbm, edge_hbm, far_hbm, msg, packet, grid_buf, edge_buf, far_buf, sems):
    chunks = grid_buf.shape[0] // CHUNK
    edge_copy = pltpu.make_async_copy(edge_hbm, edge_buf, sems.at[chunks])
    far_copy = pltpu.make_async_copy(far_hbm, far_buf, sems.at[chunks + 1])
    edge_copy.start()
    copies = []
    for c in range(chunks):
        span = pl.ds(c * CHUNK, CHUNK)
        copies.append(pltpu.make_async_copy(grid_hbm.at[span], grid_buf.at[span], sems.at[c]))
        copies[-1].start()
    far_copy.start()
    edge_copy.wait()
    for c in range(chunks):
        span = pl.ds(c * CHUNK, CHUNK)
        copies[c].wait()
        msg[span, :] = silu(dot(grid_buf[span, :], edge_buf[...])).astype(BF16)
    far_copy.wait()
    rows = far_buf.shape[1]
    for slot in range(2):
        packet[pl.ds(slot * rows, rows), :] = dot(far_buf[slot], msg[...]).astype(BF16)
    at = lax.broadcasted_iota(jnp.int32, (16, packet.shape[1]), 0)
    tags = jnp.where(at == 0, enc_codes[0], jnp.where(at == 1, enc_codes[1], jnp.where(at == 2, proc_codes[0], proc_codes[1])))
    packet[pl.ds(2 * rows, 16), :] = tags.astype(F32).astype(BF16)


def encode_near_kernel(live, msg, near, part_a, part_b, part_own, masked):
    odd = parity()
    rows = part_a.shape[0]
    for k, out in ((2 - 2 * odd, part_a), (2 * odd, part_b), (1, part_own)):
        for t in range(live.shape[1]):
            cols = pl.ds(t * rows, rows)
            masked[:, cols] = near[k, :, cols] * live[k, t].astype(F32).astype(BF16)
        out[...] = dot(masked[...], msg[...]).astype(BF16)


def line_sum_kernel(p0, p1, p2, p3, s0, s1, s2, s3, line_tags):
    packets, outs, codes = (p0, p1, p2, p3), (s0, s1, s2, s3), column_codes()
    rows = s0.shape[0]
    for p, one in enumerate(packets):
        line_tags[pl.ds(16 * p, 16), :] = one[pl.ds(2 * rows, 16), :]
    tags = [one[pl.ds(2 * rows, 16), :].astype(F32) for one in packets]
    masks = [[[(tag[slot : slot + 1] == code).astype(F32) for slot in range(2)] for tag in tags] for code in codes]

    def step(i, carry):
        at = pl.multiple_of(i * 16, 16)
        tiles = [[one[pl.ds(slot * rows + at, 16), :].astype(F32) for slot in range(2)] for one in packets]
        for out, mask in zip(outs, masks):
            terms = [mask[p][slot] * tiles[p][slot] for p in range(LINE) for slot in range(2)]
            while len(terms) > 1:
                terms = [a + b for a, b in zip(terms[::2], terms[1::2])]
            out[pl.ds(at, 16), :] = terms[0].astype(BF16)
        return carry

    lax.fori_loop(0, rows // 16, step, 0)


def mesh_kernel(own, near_a, near_b, s0, s1, s2, s3, state, first, second, edge, mid, msg):
    total = own[...].astype(F32) + near_a[...].astype(F32) + near_b[...].astype(F32)
    for s in (s0, s1, s2, s3):
        total = total + s[...].astype(F32)
    hidden = silu(dot(norm_rows(total), first[...])).astype(BF16)
    latent = (state[...].astype(F32) + dot(hidden, second[...])).astype(BF16)
    mid[...] = latent
    msg[...] = silu(dot(latent, edge[...])).astype(BF16)


def wanted_kernel(line_tags, c0, c1, c2, c3, w0, w1, w2, w3):
    column, codes = (c0, c1, c2, c3), column_codes()
    rows = c0.shape[0]
    wants = [[(tag[2 + slot : 3 + slot] == code).astype(F32) for code in codes] for tag in [line_tags[pl.ds(16 * p, 16), :].astype(F32) for p in range(LINE)] for slot in range(2)]

    def step(i, carry):
        at = pl.multiple_of(i * 16, 16)
        tiles = [tile[pl.ds(at, 16), :].astype(F32) for tile in column]
        for n, want in enumerate(wants):
            terms = [m * tile for m, tile in zip(want, tiles)]
            found = (terms[0] + terms[1]) + (terms[2] + terms[3])
            (w0, w1, w2, w3)[n // 2][pl.ds((n % 2) * rows + at, 16), :] = found.astype(BF16)
        return carry

    lax.fori_loop(0, rows // 16, step, 0)


def process_kernel(msg, near_a, near_b, w0, w1, w2, w3, mid, near, far, first, second, edge, out, dec_msg):
    odd = parity()
    rows = msg.shape[0]
    total = dot(near[1], msg[...]) + dot(near[2 - 2 * odd], near_a[...]) + dot(near[2 * odd], near_b[...])
    for slot in range(2):
        span = pl.ds(slot * rows, rows)
        picked = (w0[span, :].astype(F32) + w1[span, :].astype(F32)) + (w2[span, :].astype(F32) + w3[span, :].astype(F32))
        total = total + dot(far[slot], picked.astype(BF16))
    hidden = silu(dot(norm_rows(total), first[...])).astype(BF16)
    latent = (mid[...].astype(F32) + dot(hidden, second[...])).astype(BF16)
    out[...] = latent
    dec_msg[...] = silu(dot(latent, edge[...])).astype(BF16)


def decode_kernel(live, own, near_a, near_b, near, grid, first, second, out_hbm, masked, sources, out_buf, sems):
    odd = parity()
    rows = own.shape[0]
    chunks = grid.shape[0] // CHUNK
    order = (1, 2 - 2 * odd, 2 * odd)
    for i, source in enumerate((own, near_a, near_b)):
        sources[pl.ds(i * rows, rows), :] = source[...]
    copies = []
    for c in range(chunks):
        span = pl.ds(c * CHUNK, CHUNK)
        for t in range(c * CHUNK // rows, (c + 1) * CHUNK // rows):
            at = pl.ds(t * rows, rows)
            for i, k in enumerate(order):
                masked[at, pl.ds(i * rows, rows)] = near[k, at, :] * live[k, t].astype(F32).astype(BF16)
        total = dot(masked[span, :], sources[...])
        hidden = silu(dot(norm_rows(total), first[...])).astype(BF16)
        out_buf[span, :] = (grid[span, :].astype(F32) + dot(hidden, second[...])).astype(BF16)
        copies.append(pltpu.make_async_copy(out_buf.at[span], out_hbm.at[span], sems.at[c]))
        copies[-1].start()
    for copy in copies:
        copy.wait()


def call(kernel, outs, in_specs, scratch=(), out_specs=None, flops=0, moved=0):
    return pl.pallas_call(
        kernel,
        out_shape=outs,
        in_specs=in_specs,
        out_specs=out_specs if out_specs is not None else (VMEM,) * len(outs),
        scratch_shapes=scratch,
        compiler_params=pltpu.CompilerParams(vmem_limit_bytes=16 << 20),
        cost_estimate=pl.CostEstimate(flops=flops, bytes_accessed=moved, transcendentals=0),
    )


def body(
    grid_state,
    mesh_state,
    encode_edge,
    encode_first,
    encode_second,
    process_edge,
    process_first,
    process_second,
    decode_edge,
    decode_first,
    decode_second,
    encode_near,
    encode_live,
    encode_far,
    encode_groups,
    process_near,
    process_far,
    process_groups,
    decode_near,
    decode_live,
):
    sizes = (lax.axis_size("group"), lax.axis_size("dev"))
    rows, features = mesh_state.shape
    nodes = grid_state.shape[0]
    chunks = nodes // CHUNK
    tile = jax.ShapeDtypeStruct((rows, features), BF16)
    pair = jax.ShapeDtypeStruct((2 * rows, features), BF16)
    whole = jax.ShapeDtypeStruct((nodes, features), BF16)
    packed = jax.ShapeDtypeStruct((2 * rows + 16, features), BF16)
    dma = pltpu.SemaphoreType.DMA

    def swap(value, second, step):
        return lax.ppermute(value, AXES, line_pairs(sizes, second, step))

    def near_swap(value, far_pair):
        return lax.ppermute(value, AXES, near_pairs(sizes, far_pair))

    enc_msg, packet = call(
        encode_far_kernel,
        (whole, packed),
        [SMEM, SMEM, HBM, HBM, HBM],
        [pltpu.VMEM(grid_state.shape, BF16), pltpu.VMEM(encode_edge.shape, BF16), pltpu.VMEM(encode_far.shape, BF16), dma((chunks + 2,))],
        flops=2 * nodes * features * (features + 2 * rows),
        moved=4 << 20,
    )(encode_groups.reshape(2), process_groups.reshape(2), grid_state, encode_edge, encode_far)
    packets = [packet] + [swap(packet, False, step) for step in (1, 2, 3)]
    part_a, part_b, part_own = call(
        encode_near_kernel,
        (tile,) * 3,
        [SMEM, VMEM, VMEM],
        [pltpu.VMEM((rows, nodes), BF16)],
        flops=2 * nodes * features * 3 * rows,
        moved=2 << 20,
    )(encode_live, enc_msg, encode_near)
    near_a, near_b = near_swap(part_a, 0), near_swap(part_b, 1)
    *sums, line_tags = call(line_sum_kernel, (tile,) * 4 + (jax.ShapeDtypeStruct((16 * LINE, features), BF16),), [VMEM] * 4, flops=1 << 22, moved=2 << 20)(*packets)
    sums = [sums[0]] + [swap(sums[step], True, step) for step in (1, 2, 3)]
    mesh_mid, proc_msg = call(mesh_kernel, (tile,) * 2, [VMEM] * 11, flops=6 * rows * features * features, moved=3 << 20)(
        part_own, near_a, near_b, *sums, mesh_state, encode_first, encode_second, process_edge
    )

    column = [proc_msg] + [swap(proc_msg, True, step) for step in (1, 2, 3)]
    near_a, near_b = near_swap(proc_msg, 0), near_swap(proc_msg, 1)
    wanted = call(wanted_kernel, (pair,) * 4, [VMEM] * 5, flops=1 << 22, moved=2 << 20)(line_tags, *column)
    wanted = [wanted[0]] + [swap(wanted[step], False, step) for step in (1, 2, 3)]
    mesh_next, dec_msg = call(process_kernel, (tile,) * 2, [VMEM] * 13, flops=9 * rows * features * features, moved=4 << 20)(
        proc_msg, near_a, near_b, *wanted, mesh_mid, process_near, process_far, process_first, process_second, decode_edge
    )

    (grid_next,) = call(
        decode_kernel,
        (whole,),
        [SMEM] + [VMEM] * 7,
        [
            pltpu.VMEM((nodes, 3 * rows), BF16),
            pltpu.VMEM((3 * rows, features), BF16),
            pltpu.VMEM(grid_state.shape, BF16),
            dma((chunks,)),
        ],
        out_specs=(HBM,),
        flops=2 * nodes * features * (2 * features + 3 * rows),
        moved=5 << 20,
    )(decode_live, dec_msg, near_swap(dec_msg, 0), near_swap(dec_msg, 1), decode_near, grid_state, decode_first, decode_second)
    return (grid_next, mesh_next)


def solution(mesh):
    split = P(AXES, None)
    inner = P(None, AXES, None)
    flags = P(None, AXES)
    return jax.shard_map(
        body,
        mesh=mesh,
        in_specs=(split, split) + (P(),) * 9 + (inner, flags, inner, flags, inner, inner, flags, inner, flags),
        out_specs=(split, split),
        check_vma=False,
    )
```

```python
import jax
import jax.numpy as jnp
from jax import lax
from jax.experimental import pallas as pl
from jax.experimental.pallas import tpu as pltpu
from jax.sharding import PartitionSpec as P


AXES = ("group", "dev")
SQUARES = ((0, 1, 4, 5), (0, 3, 12, 15))


def square_pairs(axis_sizes, second, step):
    groups, devs = axis_sizes
    return [
        (region * devs + dev, (region ^ SQUARES[(dev + second) % 2][step]) * devs + dev)
        for region in range(groups)
        for dev in range(devs)
    ]


def near_pairs(axis_sizes, odd):
    groups, devs = axis_sizes
    pairs = []
    for region in range(groups):
        for dev in range(odd, devs - 1, 2):
            low = region * devs + dev
            pairs += [(low, low + 1), (low + 1, low)]
    return pairs


F32, BF16 = jnp.float32, jnp.bfloat16
VMEM = pl.BlockSpec(memory_space=pltpu.VMEM)
SMEM = pl.BlockSpec(memory_space=pltpu.SMEM)
HBM = pl.BlockSpec(memory_space=pltpu.HBM)
CHUNK = 256


def dot(a, b):
    return jnp.dot(a, b, preferred_element_type=F32)


def silu(v):
    return v * (0.5 * jnp.tanh(0.5 * v) + 0.5)


def norm_rows(v):
    centred = v - jnp.mean(v, axis=-1, keepdims=True)
    variance = jnp.mean(centred * centred, axis=-1, keepdims=True)
    return (centred * lax.rsqrt(variance + 1e-05)).astype(BF16)


def parity():
    return lax.rem(lax.axis_index("dev"), 2)


def column_codes():
    region, odd = lax.axis_index("group"), parity()
    return [
        lax.bitwise_xor(region, jnp.where(odd == 0, even_mask, odd_mask)).astype(F32)
        for even_mask, odd_mask in zip(SQUARES[1], SQUARES[0])
    ]


def encode_far_kernel(enc_codes, proc_codes, grid_hbm, edge_hbm, far_hbm, msg, packet, grid_buf, edge_buf, far_buf, sems):
    chunks = grid_buf.shape[0] // CHUNK
    edge_copy = pltpu.make_async_copy(edge_hbm, edge_buf, sems.at[chunks])
    far_copy = pltpu.make_async_copy(far_hbm, far_buf, sems.at[chunks + 1])
    edge_copy.start()
    copies = []
    for c in range(chunks):
        span = pl.ds(c * CHUNK, CHUNK)
        copies.append(pltpu.make_async_copy(grid_hbm.at[span], grid_buf.at[span], sems.at[c]))
        copies[-1].start()
    far_copy.start()
    edge_copy.wait()
    for c in range(chunks):
        span = pl.ds(c * CHUNK, CHUNK)
        copies[c].wait()
        msg[span, :] = silu(dot(grid_buf[span, :], edge_buf[...])).astype(BF16)
    far_copy.wait()
    rows = far_buf.shape[1]
    packet[pl.ds(0, 2 * rows), :] = dot(far_buf[...].reshape(2 * rows, -1), msg[...]).astype(BF16)
    at = lax.broadcasted_iota(jnp.int32, (16, packet.shape[1]), 0)
    tags = jnp.where(at == 0, enc_codes[0], jnp.where(at == 1, enc_codes[1], jnp.where(at == 2, proc_codes[0], proc_codes[1])))
    packet[pl.ds(2 * rows, 16), :] = tags.astype(F32).astype(BF16)


def encode_near_kernel(live, msg, near, part_a, part_b, part_own, masked):
    odd = parity()
    rows = part_a.shape[0]
    for i, k in enumerate((2 - 2 * odd, 2 * odd, 1)):
        for t in range(live.shape[1]):
            cols = pl.ds(t * rows, rows)
            masked[pl.ds(i * rows, rows), cols] = near[k, :, cols] * live[k, t].astype(F32).astype(BF16)
    parts = dot(masked[...], msg[...]).astype(BF16)
    for i, out in enumerate((part_a, part_b, part_own)):
        out[...] = parts[i * rows : (i + 1) * rows]


def square_sum_kernel(p0, p1, p2, p3, s0, s1, s2, s3, square_tags):
    packets, outs, codes = (p0, p1, p2, p3), (s0, s1, s2, s3), column_codes()
    rows = s0.shape[0]
    for p, one in enumerate(packets):
        square_tags[pl.ds(16 * p, 16), :] = one[pl.ds(2 * rows, 16), :]
    tags = [one[pl.ds(2 * rows, 16), :].astype(F32) for one in packets]
    masks = [[[(tag[slot : slot + 1] == code).astype(F32) for slot in range(2)] for tag in tags] for code in codes]

    def step(i, carry):
        at = pl.multiple_of(i * 16, 16)
        tiles = [[one[pl.ds(slot * rows + at, 16), :].astype(F32) for slot in range(2)] for one in packets]
        for out, mask in zip(outs, masks):
            terms = [mask[p][slot] * tiles[p][slot] for p in range(4) for slot in range(2)]
            while len(terms) > 1:
                terms = [a + b for a, b in zip(terms[::2], terms[1::2])]
            out[pl.ds(at, 16), :] = terms[0].astype(BF16)
        return carry

    lax.fori_loop(0, rows // 16, step, 0)


def mesh_kernel(own, near_a, near_b, s0, s1, s2, s3, state, first, second, edge, mid, msg):
    total = own[...].astype(F32) + near_a[...].astype(F32) + near_b[...].astype(F32)
    for s in (s0, s1, s2, s3):
        total = total + s[...].astype(F32)
    hidden = silu(dot(norm_rows(total), first[...])).astype(BF16)
    latent = (state[...].astype(F32) + dot(hidden, second[...])).astype(BF16)
    mid[...] = latent
    msg[...] = silu(dot(latent, edge[...])).astype(BF16)


def wanted_kernel(square_tags, c0, c1, c2, c3, w0, w1, w2, w3):
    column, codes = (c0, c1, c2, c3), column_codes()
    rows = c0.shape[0]
    wants = [[(tag[2 + slot : 3 + slot] == code).astype(F32) for code in codes] for tag in [square_tags[pl.ds(16 * p, 16), :].astype(F32) for p in range(4)] for slot in range(2)]

    def step(i, carry):
        at = pl.multiple_of(i * 16, 16)
        tiles = [tile[pl.ds(at, 16), :].astype(F32) for tile in column]
        for n, want in enumerate(wants):
            terms = [m * tile for m, tile in zip(want, tiles)]
            found = (terms[0] + terms[1]) + (terms[2] + terms[3])
            (w0, w1, w2, w3)[n // 2][pl.ds((n % 2) * rows + at, 16), :] = found.astype(BF16)
        return carry

    lax.fori_loop(0, rows // 16, step, 0)


def process_near_kernel(msg, near_a, near_b, near, total):
    odd = parity()
    total[...] = dot(near[1], msg[...]) + dot(near[2 - 2 * odd], near_a[...]) + dot(near[2 * odd], near_b[...])


def process_kernel(near_total, w0, w1, w2, w3, mid, far, first, second, edge, out, dec_msg):
    rows = mid.shape[0]
    total = near_total[...]
    for slot in range(2):
        span = pl.ds(slot * rows, rows)
        picked = (w0[span, :].astype(F32) + w1[span, :].astype(F32)) + (w2[span, :].astype(F32) + w3[span, :].astype(F32))
        total = total + dot(far[slot], picked.astype(BF16))
    hidden = silu(dot(norm_rows(total), first[...])).astype(BF16)
    latent = (mid[...].astype(F32) + dot(hidden, second[...])).astype(BF16)
    out[...] = latent
    dec_msg[...] = silu(dot(latent, edge[...])).astype(BF16)


def decode_own_kernel(live, own, near, total, masked):
    odd = parity()
    rows = own.shape[0]

    def flag(k, t):
        return live[k, t].astype(F32)

    for t in range(live.shape[1]):
        at = pl.ds(t * rows, rows)
        for i, k in enumerate((2 - 2 * odd, 2 * odd)):
            masked[at, pl.ds(i * rows, rows)] = near[k, at, :] * flag(k, t).astype(BF16)
        total[at, :] = dot(near[1, at, :] * flag(1, t).astype(BF16), own[...])


def decode_kernel(total, masked, near_a, near_b, grid, first, second, out_hbm, sources, out_buf, sems):
    rows = near_a.shape[0]
    sources[pl.ds(0, rows), :] = near_a[...]
    sources[pl.ds(rows, rows), :] = near_b[...]
    copies = []
    for c in range(grid.shape[0] // CHUNK):
        span = pl.ds(c * CHUNK, CHUNK)
        summed = total[span, :] + dot(masked[span, :], sources[...])
        hidden = silu(dot(norm_rows(summed), first[...])).astype(BF16)
        out_buf[span, :] = (grid[span, :].astype(F32) + dot(hidden, second[...])).astype(BF16)
        copies.append(pltpu.make_async_copy(out_buf.at[span], out_hbm.at[span], sems.at[c]))
        copies[-1].start()
    for copy in copies:
        copy.wait()


def call(kernel, outs, in_specs, scratch=(), out_specs=None, flops=0, moved=0):
    return pl.pallas_call(
        kernel,
        out_shape=outs,
        in_specs=in_specs,
        out_specs=out_specs if out_specs is not None else (VMEM,) * len(outs),
        scratch_shapes=scratch,
        compiler_params=pltpu.CompilerParams(vmem_limit_bytes=16 << 20),
        cost_estimate=pl.CostEstimate(flops=flops, bytes_accessed=moved, transcendentals=0),
    )


def step(
    grid_state,
    mesh_state,
    encode_edge,
    encode_first,
    encode_second,
    process_edge,
    process_first,
    process_second,
    decode_edge,
    decode_first,
    decode_second,
    encode_near,
    encode_live,
    encode_far,
    encode_groups,
    process_near,
    process_far,
    process_groups,
    decode_near,
    decode_live,
):
    sizes = (lax.axis_size("group"), lax.axis_size("dev"))
    rows, features = mesh_state.shape
    nodes = grid_state.shape[0]
    chunks = nodes // CHUNK
    tile = jax.ShapeDtypeStruct((rows, features), BF16)
    pair = jax.ShapeDtypeStruct((2 * rows, features), BF16)
    whole = jax.ShapeDtypeStruct((nodes, features), BF16)
    packed = jax.ShapeDtypeStruct((2 * rows + 16, features), BF16)
    dma = pltpu.SemaphoreType.DMA

    def swap(value, second, step):
        return lax.ppermute(value, AXES, square_pairs(sizes, second, step))

    def near_swap(value, far_pair):
        return lax.ppermute(value, AXES, near_pairs(sizes, far_pair))

    def in_hbm(value):
        return pltpu.with_memory_space_constraint(value, pltpu.HBM)

    enc_msg, packet = call(
        encode_far_kernel,
        (whole, packed),
        [SMEM, SMEM, HBM, HBM, HBM],
        [pltpu.VMEM(grid_state.shape, BF16), pltpu.VMEM(encode_edge.shape, BF16), pltpu.VMEM(encode_far.shape, BF16), dma((chunks + 2,))],
        flops=2 * nodes * features * (features + 2 * rows),
        moved=4 << 20,
    )(encode_groups.reshape(2), process_groups.reshape(2), in_hbm(grid_state), in_hbm(encode_edge), in_hbm(encode_far))
    packets = [packet] + [swap(packet, False, step) for step in (1, 2, 3)]
    part_a, part_b, part_own = call(
        encode_near_kernel,
        (tile,) * 3,
        [SMEM, VMEM, VMEM],
        [pltpu.VMEM((3 * rows, nodes), BF16)],
        flops=2 * nodes * features * 3 * rows,
        moved=2 << 20,
    )(encode_live, enc_msg, encode_near)
    near_a, near_b = near_swap(part_a, 0), near_swap(part_b, 1)
    *sums, square_tags = call(square_sum_kernel, (tile,) * 4 + (jax.ShapeDtypeStruct((16 * 4, features), BF16),), [VMEM] * 4, flops=1 << 22, moved=2 << 20)(*packets)
    sums = [sums[0]] + [swap(sums[step], True, step) for step in (1, 2, 3)]
    mesh_mid, proc_msg = call(mesh_kernel, (tile,) * 2, [VMEM] * 11, flops=6 * rows * features * features, moved=3 << 20)(
        part_own, near_a, near_b, *sums, mesh_state, encode_first, encode_second, process_edge
    )

    column = [proc_msg] + [swap(proc_msg, True, step) for step in (1, 2, 3)]
    near_a, near_b = near_swap(proc_msg, 0), near_swap(proc_msg, 1)
    wanted = call(wanted_kernel, (pair,) * 4, [VMEM] * 5, flops=1 << 22, moved=2 << 20)(square_tags, *column)
    wanted = [wanted[0]] + [swap(wanted[step], False, step) for step in (1, 2, 3)]
    summed = jax.ShapeDtypeStruct((rows, features), F32)
    (near_total,) = call(process_near_kernel, (summed,), [VMEM] * 4, flops=6 * rows * rows * features, moved=1 << 20)(
        proc_msg, near_a, near_b, process_near
    )
    mesh_next, dec_msg = call(process_kernel, (tile,) * 2, [VMEM] * 10, flops=9 * rows * features * features, moved=4 << 20)(
        near_total, *wanted, mesh_mid, process_far, process_first, process_second, decode_edge
    )

    near_a, near_b = near_swap(dec_msg, 0), near_swap(dec_msg, 1)
    own_total = jax.ShapeDtypeStruct((nodes, features), F32)
    masked = jax.ShapeDtypeStruct((nodes, 2 * rows), BF16)
    own_total, masked = call(
        decode_own_kernel, (own_total, masked), [SMEM, VMEM, VMEM], flops=2 * nodes * features * rows, moved=4 << 20
    )(decode_live, dec_msg, decode_near)
    (grid_next,) = call(
        decode_kernel,
        (whole,),
        [VMEM] * 7,
        [pltpu.VMEM((2 * rows, features), BF16), pltpu.VMEM(grid_state.shape, BF16), dma((chunks,))],
        out_specs=(HBM,),
        flops=2 * nodes * features * (2 * features + 2 * rows),
        moved=5 << 20,
    )(own_total, masked, near_a, near_b, grid_state, decode_first, decode_second)
    return (grid_next, mesh_next)


def solution(mesh):
    split = P(AXES, None)
    inner = P(None, AXES, None)
    flags = P(None, AXES)
    return jax.shard_map(
        step,
        mesh=mesh,
        in_specs=(split, split) + (P(),) * 9 + (inner, flags, inner, flags, inner, inner, flags, inner, flags),
        out_specs=(split, split),
        check_vma=False,
    )
```

```python
import jax
import jax.numpy as jnp
from jax import lax
from jax.experimental import pallas as pl
from jax.experimental.pallas import tpu as pltpu
from jax.sharding import PartitionSpec as P


AXES = ("group", "dev")
SQUARES = ((0, 12, 1, 13), (0, 3, 4, 7))


def square_pairs(axis_sizes, second, step):
    groups, devs = axis_sizes
    return [
        (region * devs + dev, (region ^ SQUARES[(dev + second) % 2][step]) * devs + dev)
        for region in range(groups)
        for dev in range(devs)
    ]


def near_pairs(axis_sizes, odd):
    groups, devs = axis_sizes
    pairs = []
    for region in range(groups):
        for dev in range(devs):
            other = dev + 1 if dev % 2 == odd else dev - 1
            inside = 0 <= other < devs
            pairs.append((region * devs + dev, region * devs + other if inside else (region ^ 1) * devs + dev))
    return pairs


F32, BF16 = jnp.float32, jnp.bfloat16
VMEM = pl.BlockSpec(memory_space=pltpu.VMEM)
SMEM = pl.BlockSpec(memory_space=pltpu.SMEM)
HBM = pl.BlockSpec(memory_space=pltpu.HBM)
LANES = 128
TAG_ROWS = 16
ENCODE_CHUNK = 256
DECODE_CHUNK = 256


def dot(a, b):
    return jnp.dot(a, b, preferred_element_type=F32)


def silu_of_half(h):
    return h * jnp.tanh(h) + h


def half_norm_rows(v):
    centred = v - jnp.mean(v, axis=-1, keepdims=True)
    variance = jnp.mean(centred * centred, axis=-1, keepdims=True)
    return (centred * (0.5 * lax.rsqrt(variance + 1e-05))).astype(BF16)


def parity():
    return lax.rem(lax.axis_index("dev"), 2)


def near_b_valid():
    dev = lax.axis_index("dev")
    return jnp.where((dev == 0) | (dev == lax.axis_size("dev") - 1), 0.0, 1.0).astype(F32)


def column_codes():
    region, odd = lax.axis_index("group"), parity()
    return [
        lax.bitwise_xor(region, jnp.where(odd == 0, even_mask, odd_mask)).astype(F32)
        for even_mask, odd_mask in zip(SQUARES[1], SQUARES[0])
    ]


def encode_far_kernel(enc_codes, proc_codes, grid_hbm, edge_hbm, far_hbm, proc_hbm, msg, packet, codes, grid_buf, edge, far, proc, sems):
    rows, chunks = far.shape[1], grid_buf.shape[0] // ENCODE_CHUNK
    edge_copy = pltpu.make_async_copy(edge_hbm, edge, sems.at[chunks])
    edge_copy.start()
    copies = []
    for c in range(chunks):
        span = pl.ds(c * ENCODE_CHUNK, ENCODE_CHUNK)
        copies.append(pltpu.make_async_copy(grid_hbm.at[span], grid_buf.at[span], sems.at[c]))
        copies[-1].start()
    last = [
        pltpu.make_async_copy(far_hbm, far, sems.at[chunks + 1]),
        pltpu.make_async_copy(enc_codes, codes.at[0], sems.at[chunks + 2]),
        pltpu.make_async_copy(proc_codes, codes.at[1], sems.at[chunks + 3]),
        pltpu.make_async_copy(proc_hbm, proc, sems.at[chunks + 4]),
    ]
    for copy in last:
        copy.start()
    edge_copy.wait()
    edge[...] = edge[...] * jnp.asarray(0.5, BF16)
    for c in range(chunks):
        span = pl.ds(c * ENCODE_CHUNK, ENCODE_CHUNK)
        copies[c].wait()
        msg[span, :] = silu_of_half(dot(grid_buf[span, :], edge[...])).astype(BF16)
    for copy in last:
        copy.wait()
    packet[pl.ds(0, 2 * rows), :] = dot(far[...].reshape(2 * rows, -1), msg[...]).astype(BF16)
    wide = proc[...].reshape(2 * rows, LANES)
    for part in range(4):
        lanes = pl.ds(part * LANES, LANES)
        packet[pl.ds(2 * rows, TAG_ROWS), lanes] = jnp.full((TAG_ROWS, LANES), codes[part // 2, part % 2].astype(F32)).astype(BF16)
        packet[pl.ds(2 * rows + TAG_ROWS, rows // 2), lanes] = wide[part * (rows // 2) : (part + 1) * (rows // 2)]


def encode_near_kernel(live, msg, near, part_a, part_b, part_own, masked):
    odd = parity()
    rows = part_a.shape[0]
    for i, k in enumerate((2 - 2 * odd, 2 * odd, 1)):
        for t in range(live.shape[1]):
            cols = pl.ds(t * rows, rows)
            masked[pl.ds(i * rows, rows), cols] = near[k, :, cols] * live[k, t].astype(F32).astype(BF16)
    parts = dot(masked[...], msg[...]).astype(BF16)
    for i, out in enumerate((part_a, part_b, part_own)):
        out[...] = parts[i * rows : (i + 1) * rows]


def masks_of(tag_rows, slots, codes):
    tags = [tag_rows[:, slot * LANES : (slot + 1) * LANES].astype(F32) for slot in slots]
    return [[(tag == code).astype(F32).astype(BF16) for tag in tags] for code in codes]


def tree_sum(terms):
    while len(terms) > 1:
        terms = [a + b for a, b in zip(terms[::2], terms[1::2])] + terms[len(terms) & ~1 :]
    return terms[0]


def blocks(rows, features):
    return [(pl.ds(at, 16), pl.ds(lane, LANES)) for at in range(0, rows, 16) for lane in range(0, features, LANES)]


def packet_masks(packets, rows, codes):
    return [masks_of(one[pl.ds(2 * rows, TAG_ROWS), :], (0, 1), codes) for one in packets]


def square_sums(packets, rows, masks, block):
    tiles = [[one[pl.ds(block[0].start + slot * rows, 16), block[1]] for slot in range(2)] for one in packets]
    return [
        tree_sum([tree_sum([mask[n][slot] * tile[slot] for slot in range(2)]) for mask, tile in zip(masks, tiles)])
        for n in range(len(masks[0]))
    ]


def square_sum_kernel(p0, p1, p2, p3, s1, s2, s3):
    packets, rows = (p0, p1, p2, p3), s1.shape[0]
    masks = packet_masks(packets, rows, column_codes()[1:])
    for block in blocks(*s1.shape):
        for out, value in zip((s1, s2, s3), square_sums(packets, rows, masks, block)):
            out[block] = value


def mesh_own_kernel(own, near_a, near_b, p0, p1, p2, p3, total):
    packets, rows = (p0, p1, p2, p3), own.shape[0]
    masks = packet_masks(packets, rows, column_codes()[:1])
    valid = near_b_valid()
    for block in blocks(*own.shape):
        near = own[block].astype(F32) + near_a[block].astype(F32) + near_b[block].astype(F32) * valid
        total[block] = near + square_sums(packets, rows, masks, block)[0].astype(F32)


def mesh_kernel(own_total, s1, s2, s3, state, first, second, edge, mid, msg):
    total = (own_total[...] + s1[...].astype(F32)) + (s2[...].astype(F32) + s3[...].astype(F32))
    hidden = silu_of_half(dot(half_norm_rows(total), first[...])).astype(BF16)
    latent = (state[...].astype(F32) + dot(hidden, second[...])).astype(BF16)
    mid[...] = latent
    msg[...] = silu_of_half(dot(latent * jnp.asarray(0.5, BF16), edge[...])).astype(BF16)


def place_wanted(packet, rows, codes, left, at):
    masks = masks_of(packet[pl.ds(2 * rows, TAG_ROWS), :], (2, 3), codes)
    half = rows // 2
    for j, mask in enumerate(masks):
        for part in range(2):
            for row in range(0, half, 16):
                src = pl.ds(2 * rows + TAG_ROWS + row, 16)
                left[pl.ds(at + part * half + row, 16), pl.ds(j * rows, rows)] = tree_sum(
                    [mask[slot] * packet[src, pl.ds((2 * slot + part) * LANES, LANES)] for slot in range(2)]
                )


def stack(parts, into):
    for i, part in enumerate(parts):
        into[pl.ds(i * part.shape[0], part.shape[0]), :] = part[...]


def wanted_kernel(p1, p2, p3, c0, c1, c2, c3, w1, w2, w3, left, column):
    rows, codes = c0.shape[0], column_codes()
    stack((c0, c1, c2, c3), column)
    for i, one in enumerate((p1, p2, p3)):
        place_wanted(one, rows, codes, left, i * rows)
    products = dot(left[...], column[...]).astype(BF16)
    for i, out in enumerate((w1, w2, w3)):
        out[...] = products[i * rows : (i + 1) * rows]


def process_own_kernel(p0, c0, c1, c2, c3, near_a, near_b, near, total, left, column):
    odd = parity()
    rows = c0.shape[0]
    stack((c0, c1, c2, c3), column)
    place_wanted(p0, rows, column_codes(), left, 0)
    summed = dot(left[...], column[...])
    total[...] = summed + dot(near[1], c0[...]) + dot(near[2 - 2 * odd], near_a[...]) + dot(near[2 * odd], near_b[...]) * near_b_valid()


def process_kernel(own_total, w1, w2, w3, mid, first, second, edge, out, dec_msg):
    total = (own_total[...] + w1[...].astype(F32)) + (w2[...].astype(F32) + w3[...].astype(F32))
    hidden = silu_of_half(dot(half_norm_rows(total), first[...])).astype(BF16)
    latent = (mid[...].astype(F32) + dot(hidden, second[...])).astype(BF16)
    out[...] = latent
    dec_msg[...] = silu_of_half(dot(latent * jnp.asarray(0.5, BF16), edge[...])).astype(BF16)


def decode_own_kernel(live, own, near, total, masked):
    odd = parity()
    rows = own.shape[0]

    def flag(k, t):
        return live[k, t].astype(F32)

    for t in range(live.shape[1]):
        at = pl.ds(t * rows, rows)
        for i, (k, valid) in enumerate(((2 - 2 * odd, 1.0), (2 * odd, near_b_valid()))):
            masked[at, pl.ds(i * rows, rows)] = near[k, at, :] * (flag(k, t) * valid).astype(BF16)
        total[at, :] = dot(near[1, at, :] * flag(1, t).astype(BF16), own[...])


def decode_kernel(total, masked, near_a, near_b, grid, first, second, out_hbm, sources, normed, hidden, out_buf, sems):
    rows = near_a.shape[0]
    sources[pl.ds(0, rows), :] = near_a[...]
    sources[pl.ds(rows, rows), :] = near_b[...]
    copies = []

    def sum_and_norm(span):
        normed[span, :] = half_norm_rows(total[span, :] + dot(masked[span, :], sources[...]))

    def first_layer(span):
        hidden[span, :] = silu_of_half(dot(normed[span, :], first[...])).astype(BF16)

    def second_layer(span):
        out_buf[span, :] = (grid[span, :].astype(F32) + dot(hidden[span, :], second[...])).astype(BF16)
        copies.append(pltpu.make_async_copy(out_buf.at[span], out_hbm.at[span], sems.at[len(copies)]))
        copies[-1].start()

    spans = [pl.ds(at, DECODE_CHUNK) for at in range(0, grid.shape[0], DECODE_CHUNK)]
    stages = (sum_and_norm, first_layer, second_layer)
    for time in range(len(spans) + len(stages) - 1):
        for index in (0, 1, 2):
            if 0 <= time - index < len(spans):
                stages[index](spans[time - index])
    for copy in copies:
        copy.wait()


def call(kernel, outs, in_specs, scratch=(), out_specs=None, flops=0, moved=0):
    return pl.pallas_call(
        kernel,
        out_shape=outs,
        in_specs=in_specs,
        out_specs=out_specs if out_specs is not None else (VMEM,) * len(outs),
        scratch_shapes=scratch,
        compiler_params=pltpu.CompilerParams(vmem_limit_bytes=16 << 20),
        cost_estimate=pl.CostEstimate(flops=flops, bytes_accessed=moved, transcendentals=0),
    )


def step(
    grid_state,
    mesh_state,
    encode_edge,
    encode_first,
    encode_second,
    process_edge,
    process_first,
    process_second,
    decode_edge,
    decode_first,
    decode_second,
    encode_near,
    encode_live,
    encode_far,
    encode_groups,
    process_near,
    process_far,
    process_groups,
    decode_near,
    decode_live,
):
    sizes = (lax.axis_size("group"), lax.axis_size("dev"))
    rows, features = mesh_state.shape
    nodes = grid_state.shape[0]
    enc_chunks, dec_chunks = nodes // ENCODE_CHUNK, nodes // DECODE_CHUNK
    tile = jax.ShapeDtypeStruct((rows, features), BF16)
    whole = jax.ShapeDtypeStruct((nodes, features), BF16)
    packed = jax.ShapeDtypeStruct((2 * rows + TAG_ROWS + rows // 2, features), BF16)
    dma = pltpu.SemaphoreType.DMA

    def swap(value, second, step):
        return lax.ppermute(value, AXES, square_pairs(sizes, second, step))

    def near_swap(value, far_pair):
        return lax.ppermute(value, AXES, near_pairs(sizes, far_pair))

    def in_hbm(value):
        return pltpu.with_memory_space_constraint(value, pltpu.HBM)

    enc_msg, packet = call(
        encode_far_kernel,
        (whole, packed),
        [HBM] * 6,
        [pltpu.SMEM((2, 2), jnp.int32), pltpu.VMEM(grid_state.shape, BF16), pltpu.VMEM(encode_edge.shape, BF16), pltpu.VMEM(encode_far.shape, BF16), pltpu.VMEM(process_far.shape, BF16), dma((enc_chunks + 5,))],
        flops=2 * nodes * features * (features + 2 * rows),
        moved=4 << 20,
    )(in_hbm(encode_groups.reshape(2)), in_hbm(process_groups.reshape(2)), in_hbm(grid_state), in_hbm(encode_edge), in_hbm(encode_far), in_hbm(process_far))
    packets = [packet] + [swap(packet, False, step) for step in (1, 2, 3)]
    part_a, part_b, part_own = call(
        encode_near_kernel,
        (tile,) * 3,
        [SMEM, VMEM, VMEM],
        [pltpu.VMEM((3 * rows, nodes), BF16)],
        flops=2 * nodes * features * 3 * rows,
        moved=2 << 20,
    )(encode_live, enc_msg, encode_near)
    near_a, near_b = near_swap(part_a, 0), near_swap(part_b, 1)
    sums = call(
        square_sum_kernel,
        (tile,) * 3,
        [VMEM] * 4,
        flops=1 << 22,
        moved=2 << 20,
    )(*packets)
    sums = [swap(one, True, step) for step, one in zip((1, 2, 3), sums)]
    summed = jax.ShapeDtypeStruct((rows, features), F32)
    (own_total,) = call(mesh_own_kernel, (summed,), [VMEM] * 7, flops=1 << 22, moved=2 << 20)(part_own, near_a, near_b, *packets)
    mesh_mid, proc_msg = call(mesh_kernel, (tile,) * 2, [VMEM] * 8, flops=6 * rows * features * features, moved=3 << 20)(
        own_total, *sums, mesh_state, encode_first, encode_second, process_edge
    )

    column = [proc_msg] + [swap(proc_msg, True, step) for step in (1, 2, 3)]
    near_a, near_b = near_swap(proc_msg, 0), near_swap(proc_msg, 1)
    stacked = pltpu.VMEM((4 * rows, features), BF16)
    wanted = call(
        wanted_kernel,
        (tile,) * 3,
        [VMEM] * 7,
        [pltpu.VMEM((3 * rows, 4 * rows), BF16), stacked],
        flops=24 * rows * rows * features,
        moved=2 << 20,
    )(*packets[1:], *column)
    wanted = [swap(one, False, step) for step, one in zip((1, 2, 3), wanted)]
    (own_total,) = call(
        process_own_kernel,
        (summed,),
        [VMEM] * 8,
        [pltpu.VMEM((rows, 4 * rows), BF16), stacked],
        flops=12 * rows * rows * features,
        moved=1 << 20,
    )(packet, *column, near_a, near_b, process_near)
    mesh_next, dec_msg = call(process_kernel, (tile,) * 2, [VMEM] * 8, flops=7 * rows * features * features, moved=4 << 20)(
        own_total, *wanted, mesh_mid, process_first, process_second, decode_edge
    )

    near_a, near_b = near_swap(dec_msg, 0), near_swap(dec_msg, 1)
    own_total = jax.ShapeDtypeStruct((nodes, features), F32)
    masked = jax.ShapeDtypeStruct((nodes, 2 * rows), BF16)
    own_total, masked = call(
        decode_own_kernel, (own_total, masked), [SMEM, VMEM, VMEM], flops=2 * nodes * features * rows, moved=4 << 20
    )(decode_live, dec_msg, decode_near)
    (grid_next,) = call(
        decode_kernel,
        (whole,),
        [VMEM] * 7,
        [pltpu.VMEM((2 * rows, features), BF16)] + [pltpu.VMEM(grid_state.shape, BF16)] * 3 + [dma((dec_chunks,))],
        out_specs=(HBM,),
        flops=2 * nodes * features * (2 * features + 2 * rows),
        moved=5 << 20,
    )(own_total, masked, near_a, near_b, grid_state, decode_first, decode_second)
    return (grid_next, mesh_next)


def solution(mesh):
    split = P(AXES, None)
    inner = P(None, AXES, None)
    flags = P(None, AXES)
    return jax.shard_map(
        step,
        mesh=mesh,
        in_specs=(split, split) + (P(),) * 9 + (inner, flags, inner, flags, inner, inner, flags, inner, flags),
        out_specs=(split, split),
        check_vma=False,
    )
```

```python
import jax
import jax.numpy as jnp
from jax import lax
from jax.experimental import pallas as pl
from jax.experimental.pallas import tpu as pltpu
from jax.sharding import PartitionSpec as P


AXES = ("group", "dev")
SQUARES = ((0, 12, 1, 13), (0, 3, 4, 7))


def square_pairs(axis_sizes, second, step):
    groups, devs = axis_sizes
    return [
        (region * devs + dev, (region ^ SQUARES[(dev + second) % 2][step]) * devs + dev)
        for region in range(groups)
        for dev in range(devs)
    ]


def near_pairs(axis_sizes, odd):
    groups, devs = axis_sizes
    pairs = []
    for region in range(groups):
        for dev in range(devs):
            other = dev + 1 if dev % 2 == odd else dev - 1
            inside = 0 <= other < devs
            pairs.append((region * devs + dev, region * devs + other if inside else (region ^ 1) * devs + dev))
    return pairs


F32, BF16 = jnp.float32, jnp.bfloat16
VMEM = pl.BlockSpec(memory_space=pltpu.VMEM)
SMEM = pl.BlockSpec(memory_space=pltpu.SMEM)
HBM = pl.BlockSpec(memory_space=pltpu.HBM)
LANES = 128
TAG_ROWS = 16
ENCODE_CHUNK = 512
DECODE_CHUNK = 256


def dot(a, b):
    return jnp.dot(a, b, preferred_element_type=F32)


def silu_of_half(h):
    return h * jnp.tanh(h) + h


def half_norm_rows(v):
    centred = v - jnp.mean(v, axis=-1, keepdims=True)
    variance = jnp.mean(centred * centred, axis=-1, keepdims=True)
    return (centred * (0.5 * lax.rsqrt(variance + 1e-05))).astype(BF16)


def parity():
    return lax.rem(lax.axis_index("dev"), 2)


def near_b_valid():
    dev = lax.axis_index("dev")
    return jnp.where((dev == 0) | (dev == lax.axis_size("dev") - 1), 0.0, 1.0).astype(F32)


def column_codes():
    region, odd = lax.axis_index("group"), parity()
    return [
        lax.bitwise_xor(region, jnp.where(odd == 0, even_mask, odd_mask)).astype(F32)
        for even_mask, odd_mask in zip(SQUARES[1], SQUARES[0])
    ]


def encode_far_kernel(enc_codes, proc_codes, grid_hbm, edge_hbm, far_hbm, proc_hbm, msg, packet, codes, grid_buf, edge, far, proc, sems):
    rows, chunks = far.shape[1], grid_buf.shape[0] // ENCODE_CHUNK
    edge_copy = pltpu.make_async_copy(edge_hbm, edge, sems.at[chunks])
    edge_copy.start()
    copies = []
    for c in range(chunks):
        span = pl.ds(c * ENCODE_CHUNK, ENCODE_CHUNK)
        copies.append(pltpu.make_async_copy(grid_hbm.at[span], grid_buf.at[span], sems.at[c]))
        copies[-1].start()
    last = [
        pltpu.make_async_copy(far_hbm, far, sems.at[chunks + 1]),
        pltpu.make_async_copy(enc_codes, codes.at[0], sems.at[chunks + 2]),
        pltpu.make_async_copy(proc_codes, codes.at[1], sems.at[chunks + 3]),
        pltpu.make_async_copy(proc_hbm, proc, sems.at[chunks + 4]),
    ]
    for copy in last:
        copy.start()
    edge_copy.wait()
    edge[...] = edge[...] * jnp.asarray(0.5, BF16)
    for c in range(chunks):
        span = pl.ds(c * ENCODE_CHUNK, ENCODE_CHUNK)
        copies[c].wait()
        msg[span, :] = silu_of_half(dot(grid_buf[span, :], edge[...])).astype(BF16)
    for copy in last:
        copy.wait()
    packet[pl.ds(0, 2 * rows), :] = dot(far[...].reshape(2 * rows, -1), msg[...]).astype(BF16)
    wide = proc[...].reshape(2 * rows, LANES)
    for part in range(4):
        lanes = pl.ds(part * LANES, LANES)
        packet[pl.ds(2 * rows, TAG_ROWS), lanes] = jnp.full((TAG_ROWS, LANES), codes[part // 2, part % 2].astype(F32)).astype(BF16)
        packet[pl.ds(2 * rows + TAG_ROWS, rows // 2), lanes] = wide[part * (rows // 2) : (part + 1) * (rows // 2)]


def encode_near_kernel(live, msg, near, part_a, part_b, part_own, masked):
    odd = parity()
    rows = part_a.shape[0]
    for i, k in enumerate((2 - 2 * odd, 2 * odd, 1)):
        for t in range(live.shape[1]):
            cols = pl.ds(t * rows, rows)
            masked[pl.ds(i * rows, rows), cols] = near[k, :, cols] * live[k, t].astype(F32).astype(BF16)
    parts = dot(masked[...], msg[...]).astype(BF16)
    for i, out in enumerate((part_a, part_b, part_own)):
        out[...] = parts[i * rows : (i + 1) * rows]


def masks_of(tag_rows, slots, codes):
    tags = [tag_rows[:, slot * LANES : (slot + 1) * LANES].astype(F32) for slot in slots]
    return [[(tag == code).astype(F32).astype(BF16) for tag in tags] for code in codes]


def tree_sum(terms):
    while len(terms) > 1:
        terms = [a + b for a, b in zip(terms[::2], terms[1::2])] + terms[len(terms) & ~1 :]
    return terms[0]


def blocks(rows, features):
    return [(pl.ds(at, 16), pl.ds(lane, LANES)) for at in range(0, rows, 16) for lane in range(0, features, LANES)]


def packet_masks(packets, rows, codes):
    return [masks_of(one[pl.ds(2 * rows, TAG_ROWS), :], (0, 1), codes) for one in packets]


def square_sums(packets, rows, masks, block):
    tiles = [[one[pl.ds(block[0].start + slot * rows, 16), block[1]] for slot in range(2)] for one in packets]
    return [
        tree_sum([tree_sum([mask[n][slot] * tile[slot] for slot in range(2)]) for mask, tile in zip(masks, tiles)])
        for n in range(len(masks[0]))
    ]


def square_sum_kernel(p0, p1, p2, p3, s1, s2, s3):
    packets, rows = (p0, p1, p2, p3), s1.shape[0]
    masks = packet_masks(packets, rows, column_codes()[1:])
    for block in blocks(*s1.shape):
        for out, value in zip((s1, s2, s3), square_sums(packets, rows, masks, block)):
            out[block] = value


def mesh_own_kernel(own, near_a, near_b, p0, p1, p2, p3, total):
    packets, rows = (p0, p1, p2, p3), own.shape[0]
    masks = packet_masks(packets, rows, column_codes()[:1])
    valid = near_b_valid()
    for block in blocks(*own.shape):
        near = own[block].astype(F32) + near_a[block].astype(F32) + near_b[block].astype(F32) * valid
        total[block] = near + square_sums(packets, rows, masks, block)[0].astype(F32)


def mesh_kernel(own_total, s1, s2, s3, state, first, second, edge, mid, msg):
    total = (own_total[...] + s1[...].astype(F32)) + (s2[...].astype(F32) + s3[...].astype(F32))
    hidden = silu_of_half(dot(half_norm_rows(total), first[...])).astype(BF16)
    latent = (state[...].astype(F32) + dot(hidden, second[...])).astype(BF16)
    mid[...] = latent
    msg[...] = silu_of_half(dot(latent * jnp.asarray(0.5, BF16), edge[...])).astype(BF16)


def place_wanted(packet, rows, codes, left, at):
    masks = masks_of(packet[pl.ds(2 * rows, TAG_ROWS), :], (2, 3), codes)
    half = rows // 2
    for j, mask in enumerate(masks):
        for part in range(2):
            for row in range(0, half, 16):
                src = pl.ds(2 * rows + TAG_ROWS + row, 16)
                left[pl.ds(at + part * half + row, 16), pl.ds(j * rows, rows)] = tree_sum(
                    [mask[slot] * packet[src, pl.ds((2 * slot + part) * LANES, LANES)] for slot in range(2)]
                )


def stack(parts, into):
    for i, part in enumerate(parts):
        into[pl.ds(i * part.shape[0], part.shape[0]), :] = part[...]


def wanted_kernel(p1, p2, p3, c0, c1, c2, c3, w1, w2, w3, left, column):
    rows, codes = c0.shape[0], column_codes()
    stack((c0, c1, c2, c3), column)
    for i, one in enumerate((p1, p2, p3)):
        place_wanted(one, rows, codes, left, i * rows)
    products = dot(left[...], column[...]).astype(BF16)
    for i, out in enumerate((w1, w2, w3)):
        out[...] = products[i * rows : (i + 1) * rows]


def process_own_kernel(p0, c0, c1, c2, c3, near_a, near_b, near, total, left, column):
    odd = parity()
    rows = c0.shape[0]
    stack((c0, c1, c2, c3), column)
    place_wanted(p0, rows, column_codes(), left, 0)
    summed = dot(left[...], column[...])
    total[...] = summed + dot(near[1], c0[...]) + dot(near[2 - 2 * odd], near_a[...]) + dot(near[2 * odd], near_b[...]) * near_b_valid()


def process_kernel(own_total, w1, w2, w3, mid, first, second, edge, out, dec_msg):
    total = (own_total[...] + w1[...].astype(F32)) + (w2[...].astype(F32) + w3[...].astype(F32))
    hidden = silu_of_half(dot(half_norm_rows(total), first[...])).astype(BF16)
    latent = (mid[...].astype(F32) + dot(hidden, second[...])).astype(BF16)
    out[...] = latent
    dec_msg[...] = silu_of_half(dot(latent * jnp.asarray(0.5, BF16), edge[...])).astype(BF16)


def decode_own_kernel(live, own, near, total, masked):
    odd = parity()
    rows = own.shape[0]

    def flag(k, t):
        return live[k, t].astype(F32)

    for t in range(live.shape[1]):
        at = pl.ds(t * rows, rows)
        for i, (k, valid) in enumerate(((2 - 2 * odd, 1.0), (2 * odd, near_b_valid()))):
            masked[at, pl.ds(i * rows, rows)] = near[k, at, :] * (flag(k, t) * valid).astype(BF16)
        total[at, :] = dot(near[1, at, :] * flag(1, t).astype(BF16), own[...])


def decode_kernel(total, masked, near_a, near_b, grid, first, second, mesh, out_hbm, mesh_hbm, sources, normed, hidden, out_buf, sems):
    rows = near_a.shape[0]
    sources[pl.ds(0, rows), :] = near_a[...]
    sources[pl.ds(rows, rows), :] = near_b[...]
    copies = []
    mesh_copy = pltpu.make_async_copy(mesh, mesh_hbm, sems.at[grid.shape[0] // DECODE_CHUNK])
    mesh_copy.start()

    def sum_and_norm(span):
        normed[span, :] = half_norm_rows(total[span, :] + dot(masked[span, :], sources[...]))

    def first_layer(span):
        hidden[span, :] = silu_of_half(dot(normed[span, :], first[...])).astype(BF16)

    def second_layer(span):
        out_buf[span, :] = (grid[span, :].astype(F32) + dot(hidden[span, :], second[...])).astype(BF16)
        copies.append(pltpu.make_async_copy(out_buf.at[span], out_hbm.at[span], sems.at[len(copies)]))
        copies[-1].start()

    spans = [pl.ds(at, DECODE_CHUNK) for at in range(0, grid.shape[0], DECODE_CHUNK)]
    stages = (sum_and_norm, first_layer, second_layer)
    for time in range(len(spans) + len(stages) - 1):
        for index in (0, 1, 2):
            if 0 <= time - index < len(spans):
                stages[index](spans[time - index])
    for copy in copies + [mesh_copy]:
        copy.wait()


def call(kernel, outs, in_specs, scratch=(), out_specs=None, flops=0, moved=0):
    return pl.pallas_call(
        kernel,
        out_shape=outs,
        in_specs=in_specs,
        out_specs=out_specs if out_specs is not None else (VMEM,) * len(outs),
        scratch_shapes=scratch,
        compiler_params=pltpu.CompilerParams(vmem_limit_bytes=16 << 20),
        cost_estimate=pl.CostEstimate(flops=flops, bytes_accessed=moved, transcendentals=0),
    )


def step(
    grid_state,
    mesh_state,
    encode_edge,
    encode_first,
    encode_second,
    process_edge,
    process_first,
    process_second,
    decode_edge,
    decode_first,
    decode_second,
    encode_near,
    encode_live,
    encode_far,
    encode_groups,
    process_near,
    process_far,
    process_groups,
    decode_near,
    decode_live,
):
    sizes = (lax.axis_size("group"), lax.axis_size("dev"))
    rows, features = mesh_state.shape
    nodes = grid_state.shape[0]
    enc_chunks, dec_chunks = nodes // ENCODE_CHUNK, nodes // DECODE_CHUNK
    tile = jax.ShapeDtypeStruct((rows, features), BF16)
    whole = jax.ShapeDtypeStruct((nodes, features), BF16)
    packed = jax.ShapeDtypeStruct((2 * rows + TAG_ROWS + rows // 2, features), BF16)
    dma = pltpu.SemaphoreType.DMA

    def swap(value, second, step):
        return lax.ppermute(value, AXES, square_pairs(sizes, second, step))

    def near_swap(value, far_pair):
        return lax.ppermute(value, AXES, near_pairs(sizes, far_pair))

    def in_hbm(value):
        return pltpu.with_memory_space_constraint(value, pltpu.HBM)

    enc_msg, packet = call(
        encode_far_kernel,
        (whole, packed),
        [HBM] * 6,
        [pltpu.SMEM((2, 2), jnp.int32), pltpu.VMEM(grid_state.shape, BF16), pltpu.VMEM(encode_edge.shape, BF16), pltpu.VMEM(encode_far.shape, BF16), pltpu.VMEM(process_far.shape, BF16), dma((enc_chunks + 5,))],
        flops=2 * nodes * features * (features + 2 * rows),
        moved=4 << 20,
    )(in_hbm(encode_groups.reshape(2)), in_hbm(process_groups.reshape(2)), in_hbm(grid_state), in_hbm(encode_edge), in_hbm(encode_far), in_hbm(process_far))
    packets = [packet] + [swap(packet, False, step) for step in (1, 2, 3)]
    part_a, part_b, part_own = call(
        encode_near_kernel,
        (tile,) * 3,
        [SMEM, VMEM, VMEM],
        [pltpu.VMEM((3 * rows, nodes), BF16)],
        flops=2 * nodes * features * 3 * rows,
        moved=2 << 20,
    )(encode_live, enc_msg, encode_near)
    near_a, near_b = near_swap(part_a, 0), near_swap(part_b, 1)
    sums = call(
        square_sum_kernel,
        (tile,) * 3,
        [VMEM] * 4,
        flops=1 << 22,
        moved=2 << 20,
    )(*packets)
    sums = [swap(one, True, step) for step, one in zip((1, 2, 3), sums)]
    summed = jax.ShapeDtypeStruct((rows, features), F32)
    (own_total,) = call(mesh_own_kernel, (summed,), [VMEM] * 7, flops=1 << 22, moved=2 << 20)(part_own, near_a, near_b, *packets)
    mesh_mid, proc_msg = call(mesh_kernel, (tile,) * 2, [VMEM] * 8, flops=6 * rows * features * features, moved=3 << 20)(
        own_total, *sums, mesh_state, encode_first, encode_second, process_edge
    )

    column = [proc_msg] + [swap(proc_msg, True, step) for step in (1, 2, 3)]
    near_a, near_b = near_swap(proc_msg, 0), near_swap(proc_msg, 1)
    stacked = pltpu.VMEM((4 * rows, features), BF16)
    wanted = call(
        wanted_kernel,
        (tile,) * 3,
        [VMEM] * 7,
        [pltpu.VMEM((3 * rows, 4 * rows), BF16), stacked],
        flops=24 * rows * rows * features,
        moved=2 << 20,
    )(*packets[1:], *column)
    wanted = [swap(one, False, step) for step, one in zip((1, 2, 3), wanted)]
    (own_total,) = call(
        process_own_kernel,
        (summed,),
        [VMEM] * 8,
        [pltpu.VMEM((rows, 4 * rows), BF16), stacked],
        flops=12 * rows * rows * features,
        moved=1 << 20,
    )(packet, *column, near_a, near_b, process_near)
    mesh_next, dec_msg = call(process_kernel, (tile,) * 2, [VMEM] * 8, flops=7 * rows * features * features, moved=4 << 20)(
        own_total, *wanted, mesh_mid, process_first, process_second, decode_edge
    )

    near_a, near_b = near_swap(dec_msg, 0), near_swap(dec_msg, 1)
    own_total = jax.ShapeDtypeStruct((nodes, features), F32)
    masked = jax.ShapeDtypeStruct((nodes, 2 * rows), BF16)
    own_total, masked = call(
        decode_own_kernel, (own_total, masked), [SMEM, VMEM, VMEM], flops=2 * nodes * features * rows, moved=4 << 20
    )(decode_live, dec_msg, decode_near)
    grid_next, mesh_next = call(
        decode_kernel,
        (whole, tile),
        [VMEM] * 8,
        [pltpu.VMEM((2 * rows, features), BF16)] + [pltpu.VMEM(grid_state.shape, BF16)] * 3 + [dma((dec_chunks + 1,))],
        out_specs=(HBM, HBM),
        flops=2 * nodes * features * (2 * features + 2 * rows),
        moved=5 << 20,
    )(own_total, masked, near_a, near_b, grid_state, decode_first, decode_second, mesh_next)
    return (grid_next, mesh_next)


def solution(mesh):
    split = P(AXES, None)
    inner = P(None, AXES, None)
    flags = P(None, AXES)
    return jax.shard_map(
        step,
        mesh=mesh,
        in_specs=(split, split) + (P(),) * 9 + (inner, flags, inner, flags, inner, inner, flags, inner, flags),
        out_specs=(split, split),
        check_vma=False,
    )
```
